512 devices in a mesh: ctx: 64 (over y_hi, z, x), head: 8 (over y_lo, core).
Axes of the slice: x: 4, y: 8 (y_hi: 2, y_lo: 4; y = y_hi * 4 + y_lo), z: 8, core: 2. Of those that a mesh axis runs over, the one named last changes fastest.
Arguments:
- queries: bfloat16 [32768, 1024], P('ctx', 'head'), may hold values from -5 to 5
- keys: bfloat16 [32768, 128], P('ctx'), may hold values from -4 to 4
- values: bfloat16 [32768, 128], P('ctx'), may hold values from -6 to 6
- doc_lengths: int32 [16], replicated, may hold values from 1 to 4096, 32768 in all
- span_order: int32 [128], replicated, may hold values from 0 to 127, as said below
Outputs:
- attended: bfloat16 [32768, 1024], P('ctx', 'head')
The draws below stay inside these ranges and needn't reach their ends.
Inputs may be any that keep to these rules, and one draw needn't show every extreme that they name: `span_order`: stored spans 2 i and 2 i + 1 (those of ctx index i) are pack spans i and 127-i, in either order. `doc_lengths`: the lengths sum to 32768; the longest is exactly 4096.
All inputs are finite; a program needn't handle non-finite values.
Results may differ from the reference program's by a relative error of at most 0.0044.
Values may be sent and summed in bfloat16 or wider, within the bound.
No kernel may reach another device: no remote copies, remote signals or barrier semaphores. Data moves between devices by JAX's collectives and lax.ppermute only.
A program may use at most 64 MiB of HBM per device.

```python
import math
import jax
import jax.numpy as jnp
import numpy as np
from jax import lax

HQ = 8
DH = 128
CH = 256
TOKENS = 32768
DOC_MAX = 4096
SPANS = 128
DOCS = 16


def draw_queries(key, part):
    own = jax.random.fold_in(key, 11)
    result = jnp.clip(jax.random.normal(own, (TOKENS, HQ * DH), jnp.float32), -4.0, 4.0)
    return result.astype(jnp.bfloat16)


def draw_keys(key, part):
    own = jax.random.fold_in(key, 13)
    result = jnp.clip(jax.random.normal(own, (TOKENS, DH), jnp.float32), -4.0, 4.0)
    return result.astype(jnp.bfloat16)


def draw_span_order(key, part):
    half = SPANS // 2
    index = jnp.arange(half, dtype=jnp.int32)
    flips = jax.random.randint(jax.random.fold_in(key, 17), (half,), 0, 2)
    lower = index
    upper = SPANS - 1 - index
    first = jnp.where(flips == 1, upper, lower)
    second = jnp.where(flips == 1, lower, upper)
    return jnp.stack([first, second], axis=1).reshape(SPANS).astype(jnp.int32)


def block_scale(rng, dims, shards, low, top_value):
    loudness, own = 1.0, jax.random.fold_in(rng, 6)
    for position, shards_of in shards:
        steps = jnp.exp(jax.random.uniform(jax.random.fold_in(own, position), (shards_of,), jnp.float32, low / len(shards), top_value / len(shards)))
        loudness = loudness * jnp.repeat(steps, dims[position] // shards_of).reshape([-1 if axis == position else 1 for axis in range(len(dims))])
    return loudness


def profile(amount, total, reach, slope):
    weights = [(1 << 20) // math.isqrt(grade ** slope) + 1 for grade in range(2, amount + 1)]
    surplus, holding = total - reach - (amount - 1), [1] * (amount - 1)
    while surplus > 0:
        free = [i for i in range(amount - 1) if holding[i] < reach]
        pool, budget = sum([weights[i] for i in free]), surplus
        for i in free:
            more = min(reach - holding[i], max(1, budget * weights[i] // pool), surplus)
            holding[i] = holding[i] + more
            surplus = surplus - more
    return np.array([reach] + holding)


def uneven(stream_key, number_of, total, reach, lean):
    if number_of == 2:
        one = jax.random.randint(stream_key, (), max(1, total - reach), min(reach, total - 1) + 1)
        return jnp.stack([one, total - one])
    lengths = jnp.asarray(profile(number_of, total, reach, lean), jnp.int32)
    twos = (number_of - 1) // 2
    giver, sink = lengths[1:1 + 2 * twos:2], lengths[2:2 + 2 * twos:2]
    slack = jnp.minimum(giver - 1, reach - sink)
    moved = jax.random.randint(jax.random.fold_in(stream_key, 1), (twos,), 0, 1 << 20) % (slack + 1)
    lengths = lengths.at[1:1 + 2 * twos:2].set(giver - moved).at[2:2 + 2 * twos:2].set(sink + moved)
    return lengths[jax.random.permutation(jax.random.fold_in(stream_key, 2), number_of)]


def noise(own_key, extent, scale, limit, cuts=(), kind=jnp.bfloat16):
    drawn = scale * jax.random.normal(own_key, extent, jnp.float32)
    if cuts:
        drawn = drawn * block_scale(own_key, extent, cuts, -0.22, 0.18)
    return jnp.clip(drawn, -limit, limit).astype(kind)


def setup_inputs(seed: int = 0) -> dict:
    key_list = jax.random.split(jax.random.key(seed), 6)
    queries = draw_queries(jax.random.fold_in(key_list[5], 71), 0)
    keys = draw_keys(jax.random.fold_in(key_list[5], 71), 0)
    values = noise(key_list[2], (TOKENS, DH), 1.0, 6.0, ((0, 64),))
    doc_lengths = uneven(key_list[3], DOCS, TOKENS, DOC_MAX, 1).astype(jnp.int32)
    span_order = draw_span_order(jax.random.fold_in(key_list[5], 71), 0)
    return {"queries": queries, "keys": keys, "values": values, "doc_lengths": doc_lengths, "span_order": span_order}


def reference(queries, keys, values, doc_lengths, span_order):
    rows = jnp.arange(TOKENS, dtype=jnp.int32)
    places = (span_order[rows // CH] * CH + rows % CH).astype(jnp.int32)
    ends = jnp.cumsum(doc_lengths).astype(jnp.int32)
    owners = lax.optimization_barrier(jnp.sum((places[:, None] >= ends[None, :]).astype(jnp.int32), axis=1)).astype(jnp.int32)
    query_all = queries.astype(jnp.float32).reshape(TOKENS, HQ, DH)
    key_all = keys.astype(jnp.float32)
    value_all = values.astype(jnp.float32)
    block = math.gcd(TOKENS, 512)
    scale = 1.0 / math.sqrt(DH)

    def piece(index):
        start = (index * block).astype(jnp.int32)
        query_block = lax.dynamic_slice_in_dim(query_all, start, block, 0)
        query_places = lax.dynamic_slice_in_dim(places, start, block, 0)
        query_owners = lax.dynamic_slice_in_dim(owners, start, block, 0)
        scores = jnp.einsum('qhd,kd->hqk', query_block, key_all) * scale
        visible = (query_owners[:, None] == owners[None, :]) & (places[None, :] <= query_places[:, None])
        masked = jnp.where(visible[None], scores, -1e+30)
        top = lax.optimization_barrier(jnp.max(masked, axis=2, keepdims=True))
        weights = jnp.where(visible[None], jnp.exp(masked - top), 0.0)
        total = lax.optimization_barrier(jnp.sum(weights, axis=2))
        rounded = lax.optimization_barrier(weights.astype(jnp.bfloat16)).astype(jnp.float32)
        numer = jnp.einsum('hqk,kd->hqd', rounded, value_all)
        result = numer / total[:, :, None]
        return jnp.transpose(result, (1, 0, 2)).reshape(block, HQ * DH).astype(jnp.bfloat16)
    blocks = lax.map(piece, jnp.arange(TOKENS // block, dtype=jnp.int32))
    return blocks.reshape(TOKENS, HQ * DH)
```

```python
import functools
import math

import jax
import jax.numpy as jnp
from jax import lax
from jax.experimental import pallas as pl
from jax.experimental.pallas import tpu as pltpu
from jax.sharding import Mesh
from jax.sharding import PartitionSpec as P

DH = 128
CH = 256
AXES = ("y_hi", "z", "x", "y_lo", "core")
SIZES = (2, 8, 4, 4, 2)
CTX = AXES[:3]
HEAD = AXES[3:]
PLANES = SIZES[0] * SIZES[1]
EXTRA = 16
COEF = math.log2(math.e) / math.sqrt(DH)
NEGATIVE = -1e30
FLOOR = -1e25


def device(y_hi, z, x, y_lo, core):
    return (((y_hi * SIZES[1] + z) * SIZES[2] + x) * SIZES[3] + y_lo) * SIZES[4] + core


def plane_pairs(shift):
    pairs = []
    for plane in range(PLANES):
        for x in range(4):
            for y_lo in range(4):
                for core in range(2):
                    target = (plane if core == 0 else 2 * PLANES - 1 - plane) + shift
                    if target >= 2 * PLANES:
                        continue
                    folded = target >= PLANES
                    other = 2 * PLANES - 1 - target if folded else target
                    column = 3 - x if folded and core == 0 else x
                    row = y_lo if plane // 8 == other // 8 else 3 - y_lo
                    source = device(plane // 8, plane % 8, x, y_lo, core)
                    pairs.append((source, device(other // 8, other % 8, column, row, int(folded))))
    return pairs


def shifted(block, shift):
    return lax.ppermute(block, AXES, plane_pairs(shift))


def lower_slot(order_ref, ctx_ref):
    return jnp.where(order_ref[2 * ctx_ref[0]] == ctx_ref[0], 0, 1)


def pack_kernel(ctx_ref, core_ref, plane_ref, own_ref, order_ref, q_ref, k_ref, v_ref, qs_ref, kv_ref):
    low = lower_slot(order_ref, ctx_ref)
    own = jnp.where(core_ref[0] == 0, low, 1 - low)
    start = pl.multiple_of(own * CH, CH)
    kv_ref[:CH, :] = k_ref[pl.ds(start, CH), :]
    kv_ref[CH:, :] = v_ref[pl.ds(start, CH), :]
    for flow in range(2):
        slot = pl.multiple_of((low if flow == 0 else 1 - low) * CH, CH)
        block = q_ref[pl.ds(slot, CH), :]
        for x in range(4):
            qs_ref[2 * x + flow] = block


def limits_kernel(ctx_ref, core_ref, plane_ref, own_ref, length_ref, d_ref):
    rows = lax.broadcasted_iota(jnp.int32, (CH, 1), 0)
    lanes = lax.broadcasted_iota(jnp.int32, (CH, DH), 1)
    for column in range(4):
        place = rows + CH * (4 * plane_ref[0] + column)
        start = jnp.zeros((CH, 1), jnp.int32)
        end = jnp.int32(0)
        for doc in range(length_ref.shape[0]):
            end = end + length_ref[doc]
            start = jnp.where(place >= end, end, start)
        d_ref[column] = lanes - start


def attend_kernel(ctx_ref, core_ref, plane_ref, own_ref, q_ref, d_ref, kv0, kv1, kv2, kv34, o_ref, k_all, v_all):
    for slot, ref in enumerate((kv0, kv1, kv2, kv34.at[: 2 * CH], kv34.at[2 * CH :])):
        k_all[slot] = ref[:CH, :]
        v_all[slot, :, :DH] = ref[CH:, :]
        v_all[slot, :, DH:] = jnp.ones((CH, DH), jnp.bfloat16)
    core, plane, own = core_ref[0], plane_ref[0], own_ref[0]
    causal = lax.broadcasted_iota(jnp.int32, (CH, CH), 0) >= lax.broadcasted_iota(
        jnp.int32, (CH, CH), 1
    )
    eye = lax.broadcasted_iota(jnp.int32, (DH, DH), 0) == lax.broadcasted_iota(
        jnp.int32, (DH, DH), 1
    )
    extra_row = lax.broadcasted_iota(jnp.int32, (EXTRA, DH), 0)

    def one(turn, column, slots):
        x = jnp.where(core == 0, column, 3 - column)
        half = d_ref[column]
        d = jnp.concatenate([half, half + DH], axis=1)
        masks = []
        for slot in slots:
            mask = d >= -CH * (4 * (plane - slot) + own)
            if turn == 0 and isinstance(slot, int) and slot == 0:
                mask = mask & causal
            masks.append(mask)
        for head in range(2):
            block = 2 * x + head
            q = q_ref[block]
            scores = []
            top = None
            for slot, mask in zip(slots, masks):
                score = lax.dot_general(
                    q, k_all[slot], (((1,), (1,)), ((), ())), preferred_element_type=jnp.float32
                )
                score = jnp.where(mask, score, NEGATIVE)
                scores.append(score)
                top = score if top is None else jnp.maximum(top, score)
            top = jnp.maximum(jnp.max(top, axis=1, keepdims=True), FLOOR) * COEF
            total = None
            for slot, score in zip(slots, scores):
                weight = jnp.exp2(score * COEF - top).astype(jnp.bfloat16)
                term = jnp.dot(weight, v_all[slot], preferred_element_type=jnp.float32)
                total = term if total is None else total + term
            mass = total[:, DH:]
            o_ref[block, :CH, :] = (total[:, :DH] / jnp.maximum(mass, 1e-30)).astype(jnp.bfloat16)
            level = top + jnp.log2(jnp.maximum(mass, 1e-30))
            extra = jnp.zeros((EXTRA, DH), jnp.float32)
            for group in range(2):
                line = jnp.sum(
                    jnp.where(eye, level[group * DH : (group + 1) * DH], 0.0), axis=0, keepdims=True
                )
                for piece in range(3):
                    rounded = line.astype(jnp.bfloat16).astype(jnp.float32)
                    extra = jnp.where(extra_row == 2 * piece + group, rounded, extra)
                    line = line - rounded
            o_ref[block, CH:, :] = extra.astype(jnp.bfloat16)

    one(0, own, (0, 1, 2, 3, 4))
    for turn in range(1, 4):
        column = lax.rem(own + turn, 4)
        one(turn, column, (jnp.where(column > own, 0, 4), 1, 2, 3))


def merge_kernel(ctx_ref, core_ref, plane_ref, own_ref, order_ref, r_ref, out_ref, w_ref):
    low = lower_slot(order_ref, ctx_ref)
    w_ref[...] = jnp.zeros_like(w_ref)
    for flow in range(2):
        levels = []
        for x in range(4):
            pieces = r_ref[2 * x + flow, CH:, :].astype(jnp.float32)
            levels.append(pieces[0:2] + pieces[2:4] + pieces[4:6])
        top = functools.reduce(jnp.maximum, levels)
        shares = [jnp.exp2(level - top) for level in levels]
        total = functools.reduce(jnp.add, shares)
        for x in range(4):
            at = 8 * flow + 2 * x
            w_ref[at : at + 2, :] = shares[x] / total
    columns = w_ref[...].T
    for flow in range(2):
        slot = (low if flow == 0 else 1 - low) * CH
        for group in range(2):
            rows = slice(group * DH, (group + 1) * DH)
            total = None
            for x in range(4):
                at = 8 * flow + 2 * x + group
                term = columns[:, at : at + 1] * r_ref[2 * x + flow, rows, :].astype(jnp.float32)
                total = term if total is None else total + term
            start = pl.multiple_of(slot + group * DH, DH)
            out_ref[pl.ds(start, DH), :] = total.astype(jnp.bfloat16)


def in_vmem(count):
    return [pl.BlockSpec(memory_space=pltpu.VMEM)] * count


def in_smem(count):
    return [pl.BlockSpec(memory_space=pltpu.SMEM)] * count


def struct(shape, dtype=jnp.bfloat16):
    return jax.ShapeDtypeStruct(shape, dtype)


def close(array):
    return pltpu.with_memory_space_constraint(array, pltpu.VMEM)


def body(queries, keys, values, doc_lengths, span_order):
    ctx = lax.axis_index(CTX).astype(jnp.int32)
    core = lax.axis_index("core").astype(jnp.int32)
    first = core == 0
    z_line = jnp.where(first, ctx // 4, 2 * PLANES - 1 - ctx // 4)
    column = jnp.where(first, ctx % 4, 3 - ctx % 4)
    meta = tuple(part.reshape(1) for part in (ctx, core, z_line, column))

    sent, own = pl.pallas_call(
        pack_kernel,
        out_shape=(pltpu.VMEM((8, CH, DH), jnp.bfloat16), pltpu.VMEM((2 * CH, DH), jnp.bfloat16)),
        in_specs=in_smem(5) + in_vmem(3),
        out_specs=tuple(in_vmem(2)),
        name="pack",
    )(*meta, span_order, queries, keys, values)

    near = shifted(own, 1)
    two = shifted(own, 2)
    pair = shifted(jnp.concatenate([near, two]), 2)
    asked = lax.all_to_all(sent, ("x", "core"), 0, 0, tiled=True)

    limits = pl.pallas_call(
        limits_kernel,
        out_shape=pltpu.VMEM((4, CH, DH), jnp.int32),
        in_specs=in_smem(5),
        out_specs=in_vmem(1)[0],
        cost_estimate=pl.CostEstimate(flops=4000000, bytes_accessed=600000, transcendentals=0),
        name="limits",
    )(*meta, doc_lengths)

    partial = pl.pallas_call(
        attend_kernel,
        out_shape=pltpu.VMEM((8, CH + EXTRA, DH), jnp.bfloat16),
        in_specs=in_smem(4) + in_vmem(6),
        out_specs=in_vmem(1)[0],
        scratch_shapes=[
            pltpu.VMEM((5, CH, DH), jnp.bfloat16),
            pltpu.VMEM((5, CH, 2 * DH), jnp.bfloat16),
        ],
        name="attend",
    )(*meta, *map(close, (asked, limits, own, near, two, pair)))

    back = lax.all_to_all(partial, ("x", "core"), 0, 0, tiled=True)

    return pl.pallas_call(
        merge_kernel,
        out_shape=struct((2 * CH, DH)),
        in_specs=in_smem(5) + in_vmem(1),
        out_specs=in_vmem(1)[0],
        scratch_shapes=[pltpu.VMEM((DH, DH), jnp.float32)],
        name="merge",
    )(*meta, span_order, close(back))


def solution(mesh):
    parts = Mesh(mesh.devices.reshape(SIZES), AXES)
    placed = (P(CTX, HEAD), P(CTX, None), P(CTX, None), P(), P())
    return jax.shard_map(
        body, mesh=parts, in_specs=placed, out_specs=P(CTX, HEAD), check_vma=False
    )
```

```python
import functools
import math

import jax
import jax.numpy as jnp
from jax import lax
from jax.experimental import pallas as pl
from jax.experimental.pallas import tpu as pltpu
from jax.sharding import Mesh
from jax.sharding import PartitionSpec as P


DH = 128
CH = 256
AXES = ("y_hi", "z", "x", "y_lo", "core")
SIZES = (2, 8, 4, 4, 2)
CTX = AXES[:3]
HEAD = AXES[3:]
PLANES = SIZES[0] * SIZES[1]
EXTRA = 16
COEF = math.log2(math.e) / math.sqrt(DH)
NEGATIVE = -1e30
FLOOR = -1e25


def device(y_hi, z, x, y_lo, core):
    return (((y_hi * SIZES[1] + z) * SIZES[2] + x) * SIZES[3] + y_lo) * SIZES[4] + core


def plane_pairs(shift):
    pairs = []
    for plane in range(PLANES):
        for x in range(4):
            for y_lo in range(4):
                for core in range(2):
                    target = (plane if core == 0 else 2 * PLANES - 1 - plane) + shift
                    if target >= 2 * PLANES:
                        continue
                    folded = target >= PLANES
                    other = 2 * PLANES - 1 - target if folded else target
                    column = 3 - x if folded and core == 0 else x
                    row = y_lo if plane // 8 == other // 8 else (y_lo ^ 2 if shift == 1 else 3 - y_lo)
                    source = device(plane // 8, plane % 8, x, y_lo, core)
                    pairs.append((source, device(other // 8, other % 8, column, row, int(folded))))
    return pairs


def shifted(block, shift):
    return lax.ppermute(block, AXES, plane_pairs(shift))


def lower_slot(order_ref, ctx_ref):
    return jnp.where(order_ref[2 * ctx_ref[0]] == ctx_ref[0], 0, 1)


def pack_kernel(
    ctx_ref, core_ref, plane_ref, own_ref, order_ref, q_ref, k_ref, v_ref, q_out, kv_out
):
    low = lower_slot(order_ref, ctx_ref)
    own = jnp.where(core_ref[0] == 0, low, 1 - low)
    start = pl.multiple_of(own * CH, CH)
    kv_out[:CH, :] = k_ref[pl.ds(start, CH), :]
    kv_out[CH:, :] = v_ref[pl.ds(start, CH), :]
    q_out[0] = q_ref[pl.ds(pl.multiple_of(low * CH, CH), CH), :]
    q_out[1] = q_ref[pl.ds(pl.multiple_of((1 - low) * CH, CH), CH), :]


def limits_kernel(ctx_ref, core_ref, plane_ref, own_ref, length_ref, d_ref):
    rows = lax.broadcasted_iota(jnp.int32, (CH, 1), 0)
    lanes = lax.broadcasted_iota(jnp.int32, (CH, DH), 1)
    for column in range(4):
        place = rows + CH * (4 * plane_ref[0] + column)
        start = jnp.zeros((CH, 1), jnp.int32)
        end = jnp.int32(0)
        for doc in range(length_ref.shape[0]):
            end = end + length_ref[doc]
            start = jnp.where(place >= end, end, start)
        d_ref[column] = lanes - start


def load_keys(refs, k_all, v_all):
    for slot, ref in enumerate(refs):
        k_all[slot] = ref[:CH, :]
        v_all[slot, :, :DH] = ref[CH:, :]
        v_all[slot, :, DH:] = jnp.ones((CH, DH), jnp.bfloat16)


def weigh(q, pieces, top, total):
    scores = []
    best = None
    for key, _, mask in pieces:
        score = lax.dot_general(
            q, key, (((1,), (1,)), ((), ())), preferred_element_type=jnp.float32
        )
        score = jnp.where(mask, score, NEGATIVE)
        scores.append(score)
        best = score if best is None else jnp.maximum(best, score)
    best = jnp.maximum(jnp.max(best, axis=1, keepdims=True), FLOOR) * COEF
    if top is not None:
        best = jnp.maximum(best, top)
        factor = jnp.exp2(top - best)
        total = total * jnp.concatenate([factor, factor], axis=1)
        wide = jnp.concatenate([best, best], axis=1)
    else:
        wide = best
    for (_, value, _), score in zip(pieces, scores):
        weight = jnp.exp2(score * COEF - wide).astype(jnp.bfloat16)
        term = jnp.dot(weight, value, preferred_element_type=jnp.float32)
        total = term if total is None else total + term
    return best, total


def bounds(d_ref, column):
    half = d_ref[column]
    return jnp.concatenate([half, half + DH], axis=1)


def begin_kernel(
    ctx_ref, core_ref, plane_ref, own_ref, q_ref, d_ref, kv0, kv1, kv2, top_ref, sum_ref, k_all, v_all
):
    load_keys((kv0, kv1, kv2), k_all, v_all)
    core, plane, own = core_ref[0], plane_ref[0], own_ref[0]
    causal = lax.broadcasted_iota(jnp.int32, (CH, CH), 0) >= lax.broadcasted_iota(
        jnp.int32, (CH, CH), 1
    )
    for turn in range(4):
        column = lax.rem(own + turn, 4)
        x = jnp.where(core == 0, column, 3 - column)
        d = bounds(d_ref, column)
        masks = [(slot, d >= -CH * (4 * (plane - slot) + own)) for slot in range(3)]
        if turn == 0:
            masks[0] = (0, masks[0][1] & causal)
        else:
            masks = masks[1:]
        for head in range(2):
            block = 2 * x + head
            pieces = [(k_all[slot], v_all[slot], mask) for slot, mask in masks]
            best, total = weigh(q_ref[block], pieces, None, None)
            top_ref[block] = jnp.broadcast_to(best, (CH, DH))
            sum_ref[block] = total


def finish_kernel(
    ctx_ref, core_ref, plane_ref, own_ref, q_ref, d_ref, kv0, pair, top_ref, sum_ref, o_ref, k_all, v_all
):
    load_keys((kv0, pair.at[: 2 * CH], pair.at[2 * CH :]), k_all, v_all)
    core, plane, own = core_ref[0], plane_ref[0], own_ref[0]
    eye = lax.broadcasted_iota(jnp.int32, (DH, DH), 0) == lax.broadcasted_iota(
        jnp.int32, (DH, DH), 1
    )
    extra_row = lax.broadcasted_iota(jnp.int32, (EXTRA, DH), 0)
    for turn in range(4):
        column = lax.rem(own + turn, 4)
        x = jnp.where(core == 0, column, 3 - column)
        d = bounds(d_ref, column)
        edge = jnp.where(column > own, 0, 2)
        age = jnp.where(column > own, 0, 4)
        masks = [
            (1, d >= -CH * (4 * (plane - 3) + own)),
            (edge, d >= -CH * (4 * (plane - age) + own)),
        ]
        for head in range(2):
            block = 2 * x + head
            pieces = [(k_all[slot], v_all[slot], mask) for slot, mask in masks]
            top, total = weigh(q_ref[block], pieces, top_ref[block], sum_ref[block])
            mass = jnp.maximum(total[:, DH:], 1e-30)
            o_ref[block, :CH, :] = (total[:, :DH] / mass).astype(jnp.bfloat16)
            level = top + jnp.log2(mass)
            extra = jnp.zeros((EXTRA, DH), jnp.float32)
            for group in range(2):
                line = jnp.sum(
                    jnp.where(eye, level[group * DH : (group + 1) * DH], 0.0), axis=0, keepdims=True
                )
                for piece in range(3):
                    rounded = line.astype(jnp.bfloat16).astype(jnp.float32)
                    extra = jnp.where(extra_row == 2 * piece + group, rounded, extra)
                    line = line - rounded
            o_ref[block, CH:, :] = extra.astype(jnp.bfloat16)


def merge_kernel(ctx_ref, core_ref, plane_ref, own_ref, order_ref, r_ref, out_ref, w_ref):
    low = lower_slot(order_ref, ctx_ref)
    w_ref[...] = jnp.zeros_like(w_ref)
    for flow in range(2):
        levels = []
        for x in range(4):
            pieces = r_ref[2 * x + flow, CH:, :].astype(jnp.float32)
            levels.append(pieces[0:2] + pieces[2:4] + pieces[4:6])
        top = functools.reduce(jnp.maximum, levels)
        shares = [jnp.exp2(level - top) for level in levels]
        total = functools.reduce(jnp.add, shares)
        for x in range(4):
            at = 8 * flow + 2 * x
            w_ref[at : at + 2, :] = shares[x] / total
    columns = w_ref[...].T
    for flow in range(2):
        slot = (low if flow == 0 else 1 - low) * CH
        for group in range(2):
            rows = slice(group * DH, (group + 1) * DH)
            total = None
            for x in range(4):
                at = 8 * flow + 2 * x + group
                term = columns[:, at : at + 1] * r_ref[2 * x + flow, rows, :].astype(jnp.float32)
                total = term if total is None else total + term
            start = pl.multiple_of(slot + group * DH, DH)
            out_ref[pl.ds(start, DH), :] = total.astype(jnp.bfloat16)


def in_vmem(count):
    return [pl.BlockSpec(memory_space=pltpu.VMEM)] * count


def in_smem(count):
    return [pl.BlockSpec(memory_space=pltpu.SMEM)] * count


def struct(shape, dtype=jnp.bfloat16):
    return jax.ShapeDtypeStruct(shape, dtype)


def close(array):
    return pltpu.with_memory_space_constraint(array, pltpu.VMEM)


def body(queries, keys, values, doc_lengths, span_order):
    ctx = lax.axis_index(CTX).astype(jnp.int32)
    core = lax.axis_index("core").astype(jnp.int32)
    first = core == 0
    z_line = jnp.where(first, ctx // 4, 2 * PLANES - 1 - ctx // 4)
    column = jnp.where(first, ctx % 4, 3 - ctx % 4)
    meta = tuple(part.reshape(1) for part in (ctx, core, z_line, column))

    both, own = pl.pallas_call(
        pack_kernel,
        out_shape=(pltpu.VMEM((2, CH, DH), jnp.bfloat16), pltpu.VMEM((2 * CH, DH), jnp.bfloat16)),
        in_specs=in_smem(5) + in_vmem(3),
        out_specs=tuple(in_vmem(2)),
        name="pack",
    )(*meta, span_order, queries, keys, values)

    near = shifted(own, 1)
    two = shifted(own, 2)
    sent = jnp.broadcast_to(both[None], (4, 2, CH, DH)).reshape(8, CH, DH)
    asked = lax.all_to_all(sent, ("x", "core"), 0, 0, tiled=True)
    pair = shifted(jnp.concatenate([near, two]), 2)

    limits = pl.pallas_call(
        limits_kernel,
        out_shape=pltpu.VMEM((4, CH, DH), jnp.int32),
        in_specs=in_smem(5),
        out_specs=in_vmem(1)[0],
        cost_estimate=pl.CostEstimate(flops=4000000, bytes_accessed=600000, transcendentals=0),
        name="limits",
            compiler_params=pltpu.CompilerParams(vmem_limit_bytes=24 << 20),
    )(*meta, doc_lengths)

    def keys_scratch():
        return [
            pltpu.VMEM((3, CH, DH), jnp.bfloat16),
            pltpu.VMEM((3, CH, 2 * DH), jnp.bfloat16),
        ]

    tops, sums = pl.pallas_call(
        begin_kernel,
        out_shape=(pltpu.VMEM((8, CH, DH), jnp.float32), pltpu.VMEM((8, CH, 2 * DH), jnp.float32)),
        in_specs=in_smem(4) + in_vmem(5),
        out_specs=tuple(in_vmem(2)),
        scratch_shapes=keys_scratch(),
        cost_estimate=pl.CostEstimate(flops=1000000000, bytes_accessed=1000000, transcendentals=1200000),
        name="begin",
        compiler_params=pltpu.CompilerParams(vmem_limit_bytes=24 << 20),
    )(*meta, *map(close, (asked, limits, own, near, two)))

    partial = pl.pallas_call(
        finish_kernel,
        out_shape=pltpu.VMEM((8, CH + EXTRA, DH), jnp.bfloat16),
        in_specs=in_smem(4) + in_vmem(6),
        out_specs=in_vmem(1)[0],
        scratch_shapes=keys_scratch(),
        name="finish",
            compiler_params=pltpu.CompilerParams(vmem_limit_bytes=24 << 20),
    )(*meta, *map(close, (asked, limits, own, pair, tops, sums)))

    back = lax.all_to_all(partial, ("x", "core"), 0, 0, tiled=True)

    return pl.pallas_call(
        merge_kernel,
        out_shape=struct((2 * CH, DH)),
        in_specs=in_smem(5) + in_vmem(1),
        out_specs=in_vmem(1)[0],
        scratch_shapes=[pltpu.VMEM((DH, DH), jnp.float32)],
        name="merge",
    )(*meta, span_order, close(back))


def solution(mesh):
    parts = Mesh(mesh.devices.reshape(SIZES), AXES)
    placed = (P(CTX, HEAD), P(CTX, None), P(CTX, None), P(), P())
    return jax.shard_map(body, mesh=parts, in_specs=placed, out_specs=P(CTX, HEAD), check_vma=False)
```
